768 devices in a mesh: pool: 8 (over y_hi, core), col: 96 (over x, z, y_lo).
Axes of the slice: x: 4, y: 8 (y_hi: 4, y_lo: 2; y = y_hi * 2 + y_lo), z: 12, core: 2. Of those that a mesh axis runs over, the one named last changes fastest.
Arguments:
- pair_matrix: bfloat16 [2048, 12288], P('pool', 'col'), may hold values from -1.1953125 to 1.1953125
- band_energy: float32 [8, 4, 4096], P('pool'), may hold values from -2 to 2
- occupation: int32 [8, 4, 4096], P('pool'), may hold values 0 or 1
- pair_first: int32 [8, 256], P('pool'), may hold values from 0 to 4095
- pair_second: int32 [8, 256], P('pool'), may hold values from 0 to 4095
- pair_kpoint: int32 [8, 256], P('pool'), may hold values from 0 to 3
Outputs:
- chi_zero: float32 [12288, 12288], P('pool', 'col')
The draws below stay inside these ranges and needn't reach their ends.
All inputs are finite; a program needn't handle non-finite values. No bound on the sum of `occupation` on one device may be relied on, other than what follows from the above.
Results may differ from the reference program's by a relative error of at most 0.012.
Values may be sent and summed in bfloat16 or wider, within the bound.
No kernel may reach another device: no remote copies, remote signals or barrier semaphores. Data moves between devices by JAX's collectives and lax.ppermute only.
A program may use at most 32 MiB of HBM per device.

```python
import jax
import jax.numpy as jnp
from jax import lax

NG = 12288
NBANDS = 4096
KPTS = 4
PAIRS = 256
PAIRS_ALL = 2048
N_POOL = 8


def plant(entries, key, least, largest):
    longest = entries.shape.index(max(entries.shape))
    spots = []
    for shift in (0, 1):
        where = [jax.random.randint(jax.random.fold_in(key, axis), (), 0, length) for axis, length in enumerate(entries.shape)]
        where[longest] = (where[longest] + shift) % entries.shape[longest]
        spots.append(tuple(where))
    return entries.at[spots[0]].set(least).at[spots[1]].set(largest)


def block_scale(own_key, extent, cuts, low, largest):
    factor_of = 1.0
    for axis_at, parts in cuts:
        steps = jax.random.uniform(jax.random.fold_in(jax.random.fold_in(own_key, 6), axis_at), (parts,), jnp.float32, low / len(cuts), largest / len(cuts))
        factor_of = factor_of * jnp.repeat(jnp.exp(steps), extent[axis_at] // parts).reshape((-1,) + (1,) * (len(extent) - 1 - axis_at))
    return factor_of


def scatter_about(key, extent, spread, reach, pieces=(), kind=jnp.bfloat16):
    loudness = block_scale(key, extent, pieces, -0.22, 0.18) if pieces else 1.0
    array = jax.random.normal(key, extent, jnp.float32) * spread * loudness
    return jnp.minimum(jnp.maximum(array, -reach), reach).astype(kind)


def setup_inputs(seed: int = 0) -> dict:
    streams_of = jax.random.split(jax.random.key(seed), 7)
    pair_matrix = scatter_about(streams_of[0], (PAIRS_ALL, NG), 0.2, 1.1953125, ((0, 8), (1, 96)))
    band_energy = jnp.clip(jax.random.uniform(streams_of[1], (N_POOL, KPTS, NBANDS), jnp.float32, -2.0, 2.0) * block_scale(streams_of[1], (N_POOL, KPTS, NBANDS), ((0, 8),), -0.4, 0.0), -2.0, 2.0)
    occupation = plant((jax.random.randint(streams_of[2], (N_POOL, KPTS, NBANDS), 0, 2) < 1).astype(jnp.int32), jax.random.fold_in(streams_of[2], 1), 0, 1)
    pair_first = plant(jax.random.randint(streams_of[3], (N_POOL, PAIRS), 0, NBANDS), jax.random.fold_in(streams_of[3], 1), 0, NBANDS - 1).astype(jnp.int32)
    pair_second = plant(jax.random.randint(streams_of[4], (N_POOL, PAIRS), 0, NBANDS), jax.random.fold_in(streams_of[4], 1), 0, NBANDS - 1).astype(jnp.int32)
    pair_kpoint = plant(jax.random.randint(streams_of[5], (N_POOL, PAIRS), 0, KPTS), jax.random.fold_in(streams_of[5], 1), 0, KPTS - 1).astype(jnp.int32)
    return dict(pair_matrix=pair_matrix, band_energy=band_energy, occupation=occupation, pair_first=pair_first, pair_second=pair_second, pair_kpoint=pair_kpoint)


def pool_weight(energy, occupied, first, second, kpoint):
    flat_energy = energy.reshape(-1)
    flat_occupied = occupied.reshape(-1).astype(jnp.float32)
    index_first = (kpoint * NBANDS + first).astype(jnp.int32)
    index_second = (kpoint * NBANDS + second).astype(jnp.int32)
    gap = jnp.abs(jnp.take(flat_energy, index_second) - jnp.take(flat_energy, index_first))
    filled = jnp.take(flat_occupied, index_first) - jnp.take(flat_occupied, index_second)
    return 2.0 * filled / (1.0 + gap)


def reference(pair_matrix, band_energy, occupation, pair_first, pair_second, pair_kpoint):
    total = jnp.zeros((NG, NG), jnp.float32)
    for pool_index in range(N_POOL):
        weight = pool_weight(band_energy[pool_index], occupation[pool_index], pair_first[pool_index], pair_second[pool_index], pair_kpoint[pool_index])
        block = pair_matrix[pool_index * PAIRS:(pool_index + 1) * PAIRS]
        scaled = (block.astype(jnp.float32) * weight[:, None]).astype(jnp.bfloat16)
        part = lax.dot_general(block, scaled, (((0,), (0,)), ((), ())), preferred_element_type=jnp.float32)
        total = total + part.astype(jnp.bfloat16).astype(jnp.float32)
    return total
```

```python
import jax
import jax.numpy as jnp
from jax import lax
from jax.experimental import pallas as pl
from jax.experimental.pallas import tpu as pltpu
from jax.sharding import PartitionSpec as P

H, K, X, Z, L = 4, 2, 4, 12, 2
COLS = X * Z * L
PAIRS, WIDTH = 256, 128
AXES = ("pool", "col")


def at(h, k, x, z, l):
    return ((h % H) * K + k) * COLS + (x % X) * (Z * L) + (z % Z) * L + l


def table(f):
    return [
        (at(h, k, x, z, l), at(*f(h, k, x, z, l)))
        for h in range(H)
        for k in range(K)
        for x in range(X)
        for z in range(Z)
        for l in range(L)
    ]


def move(value, f):
    return lax.ppermute(value, AXES, table(f))


Z_GROUPS = [[x * Z * L + z * L + l for z in range(Z)] for x in range(X) for l in range(L)]


def scale_kernel(energy, occupied, first, second, kpoint, block, out, energies, filled):
    chunks = energy.shape[-1] // WIDTH
    kpts = energy.shape[-2]
    for c in range(chunks):
        part = pl.ds(c * WIDTH, WIDTH)
        energies[pl.ds(c * kpts, kpts), :] = energy[0, :, part]
        filled[pl.ds(c * kpts, kpts), :] = occupied[0, :, part].astype(jnp.float32)

    def pick(table_ref, band):
        entries = table_ref.shape[0]
        place = (band // WIDTH) * kpts + kpoint[...]
        spot = band % WIDTH
        pairs = band.shape[-1]
        one = (lax.broadcasted_iota(jnp.int32, (entries, pairs), 0) == place).astype(jnp.float32)
        found = lax.dot_general(
            table_ref[...],
            one,
            (((0,), (0,)), ((), ())),
            precision=lax.Precision.HIGHEST,
            preferred_element_type=jnp.float32,
        )
        keep = lax.broadcasted_iota(jnp.int32, (WIDTH, pairs), 0) == spot
        return jnp.sum(jnp.where(keep, found, 0.0), axis=0, keepdims=True)

    a, b = first[...], second[...]
    gap = jnp.abs(pick(energies, b) - pick(energies, a))
    change = pick(filled, a) - pick(filled, b)
    weight = 2.0 * change / (1.0 + gap)
    for i in range(PAIRS // WIDTH):
        rows = pl.ds(i * WIDTH, WIDTH)
        factor = jnp.broadcast_to(weight[:, i * WIDTH : (i + 1) * WIDTH], (WIDTH, WIDTH)).T
        out[rows, :] = (block[rows, :].astype(jnp.float32) * factor).astype(jnp.bfloat16)


def scaled_block(energy, occupied, first, second, kpoint, block):
    entries = energy.shape[1] * energy.shape[2] // WIDTH
    return pl.pallas_call(
        scale_kernel,
        out_shape=jax.ShapeDtypeStruct(block.shape, jnp.bfloat16),
        scratch_shapes=[pltpu.VMEM((entries, WIDTH), jnp.float32)] * 2,
        cost_estimate=pl.CostEstimate(flops=4 * 10**8, bytes_accessed=3 * 10**5, transcendentals=0),
        name="scale",
    )(energy, occupied, first, second, kpoint, block)


def product_kernel(place, rows, c0, c1, c2, c3, out):
    pieces = [jnp.concatenate([rows[3 * s + j] for s in range(H)], axis=0) for j in range(3)]
    left = jnp.concatenate(pieces, axis=1)
    right = jnp.concatenate([c[0] for c in (c0, c1, c2, c3)], axis=1)
    found = lax.dot_general(
        left, right, (((0,), (0,)), ((), ())), preferred_element_type=jnp.float32
    )
    for i in range(X):
        out[(i + place[1]) % X] = found[:, i * WIDTH : (i + 1) * WIDTH].astype(out.dtype)


def product(side, turn, rows, columns, dtype, name):
    depth = columns[0].shape[1]
    place = jnp.stack([side, turn]).astype(jnp.int32)
    return pl.pallas_call(
        product_kernel,
        out_shape=jax.ShapeDtypeStruct((X, 3 * WIDTH, WIDTH), dtype),
        grid_spec=pltpu.PrefetchScalarGridSpec(
            num_scalar_prefetch=1,
            grid=(1,),
            in_specs=[pl.BlockSpec(rows.shape, lambda i, p: (0, 0, 0))]
            + [pl.BlockSpec((1, depth, WIDTH), lambda i, p: (p[0], 0, 0))] * X,
            out_specs=pl.BlockSpec((X, 3 * WIDTH, WIDTH), lambda i, p: (0, 0, 0)),
        ),
        cost_estimate=pl.CostEstimate(flops=4 * 10**8, bytes_accessed=3 * 10**6, transcendentals=0),
        name=name,
    )(place, rows, *columns)


def assemble_kernel(order, f0, f1, f2, f3, out):
    for i, piece in enumerate((f0, f1, f2, f3)):
        t = order[i]
        for j in range(3):
            out[t % 2, j, t // 2] = piece[j * WIDTH : (j + 1) * WIDTH, :].astype(jnp.float32)


def assemble(order, pieces):
    return pl.pallas_call(
        assemble_kernel,
        out_shape=jax.ShapeDtypeStruct((2, 3, 2, WIDTH, WIDTH), jnp.float32),
        in_specs=[pl.BlockSpec(memory_space=pltpu.SMEM)] + [pl.BlockSpec(memory_space=pltpu.VMEM)] * 4,
        out_specs=pl.BlockSpec(memory_space=pltpu.VMEM),
        name="assemble",
    )(order, *pieces)


def per_device(pair_matrix, band_energy, occupation, pair_first, pair_second, pair_kpoint):
    pool, col = lax.axis_index("pool"), lax.axis_index("col")
    k, x, l = pool % K, col // (Z * L), col % L

    around = [
        move(pair_matrix, lambda h, k, x, z, l, s=s: (h - s, k, x, z, l)) for s in range(1, H)
    ]
    scaled = scaled_block(
        band_energy, occupation, pair_first, pair_second, pair_kpoint, pair_matrix
    )
    sent = move(
        scaled, lambda h, k, x, z, l: (x, k, z // 3, 3 * ((h - x) % H) + z % 3, l)
    )
    own = jnp.concatenate([pair_matrix] + around, axis=0)
    other = move(own, lambda h, k, x, z, l: (h, k, x, z, 1 - l))
    both = jnp.stack([own, other])
    columns = [both] + [
        move(both, lambda h, k, x, z, l, s=s: (h, k, x - s, z, l)) for s in range(1, X)
    ]
    rows = lax.all_gather(sent, "col", axis=0, axis_index_groups=Z_GROUPS)

    turn = 2 * l
    give = product(1 - k, turn, rows, columns, jnp.bfloat16, "give")
    taken = move(give, lambda h, k, x, z, l: (h, 1 - k, x, z, l))
    keep = product(k, turn, rows, columns, jnp.float32, "keep")
    total = (keep + taken.astype(jnp.float32)).astype(jnp.bfloat16)
    home = [
        move(total[r], lambda h, k, x, z, l, r=r: (h, x // 2, x + r + 2 * l, z, l ^ k))
        for r in range(X)
    ]
    order = (x - 2 * k - jnp.arange(X, dtype=jnp.int32)) % X
    return assemble(order.astype(jnp.int32), home).reshape(-1, WIDTH)


def solution(mesh):
    return jax.shard_map(
        per_device,
        mesh=mesh,
        in_specs=(
            P("pool", "col"),
            P("pool", None, None),
            P("pool", None, None),
            P("pool", None),
            P("pool", None),
            P("pool", None),
        ),
        out_specs=P("pool", "col"),
        check_vma=False,
    )
```

```python
import functools

import jax
import jax.numpy as jnp
from jax import lax
from jax.experimental import pallas as pl
from jax.experimental.pallas import tpu as pltpu
from jax.sharding import PartitionSpec as P


H, K, X, Z, L = 4, 2, 4, 12, 2
COLS = X * Z * L
PAIRS, WIDTH = 256, 128
AXES = ("pool", "col")
SHIFT = (2, 1, 0, 3)


def at(h, k, x, z, l):
    return ((h % H) * K + k) * COLS + (x % X) * (Z * L) + (z % Z) * L + l


def table(f):
    return [
        (at(h, k, x, z, l), at(*f(h, k, x, z, l)))
        for h in range(H)
        for k in range(K)
        for x in range(X)
        for z in range(Z)
        for l in range(L)
    ]


def move(value, f):
    return lax.ppermute(value, AXES, table(f))


Z_GROUPS = [[x * Z * L + z * L + l for z in range(Z)] for x in range(X) for l in range(L)]


def scale_kernel(energy, occupied, first, second, kpoint, block, out, energies, filled):
    chunks = energy.shape[-1] // WIDTH
    kpts = energy.shape[-2]
    for c in range(chunks):
        part = pl.ds(c * WIDTH, WIDTH)
        energies[pl.ds(c * kpts, kpts), :] = energy[0, :, part]
        filled[pl.ds(c * kpts, kpts), :] = occupied[0, :, part].astype(jnp.float32)

    def pick(table_ref, band):
        entries = table_ref.shape[0]
        place = (band // WIDTH) * kpts + kpoint[...]
        spot = band % WIDTH
        pairs = band.shape[-1]
        one = (lax.broadcasted_iota(jnp.int32, (entries, pairs), 0) == place).astype(jnp.float32)
        found = lax.dot_general(
            table_ref[...],
            one,
            (((0,), (0,)), ((), ())),
            precision=lax.Precision.HIGHEST,
            preferred_element_type=jnp.float32,
        )
        keep = lax.broadcasted_iota(jnp.int32, (WIDTH, pairs), 0) == spot
        return jnp.sum(jnp.where(keep, found, 0.0), axis=0, keepdims=True)

    a, b = first[...], second[...]
    gap = jnp.abs(pick(energies, b) - pick(energies, a))
    change = pick(filled, a) - pick(filled, b)
    weight = 2.0 * change / (1.0 + gap)
    for i in range(PAIRS // WIDTH):
        rows = pl.ds(i * WIDTH, WIDTH)
        factor = jnp.broadcast_to(weight[:, i * WIDTH : (i + 1) * WIDTH], (WIDTH, WIDTH)).T
        out[rows, :] = (block[rows, :].astype(jnp.float32) * factor).astype(jnp.bfloat16)


def scaled_block(energy, occupied, first, second, kpoint, block):
    entries = energy.shape[1] * energy.shape[2] // WIDTH
    return pl.pallas_call(
        scale_kernel,
        out_shape=jax.ShapeDtypeStruct(block.shape, jnp.bfloat16),
        scratch_shapes=[pltpu.VMEM((entries, WIDTH), jnp.float32)] * 2,
        cost_estimate=pl.CostEstimate(flops=4 * 10**8, bytes_accessed=3 * 10**5, transcendentals=0),
        name="scale",
    )(energy, occupied, first, second, kpoint, block)


def product_kernel(side, place, rows, c0, c1, c2, c3, out):
    which = place[side]
    left = jnp.concatenate(
        [
            jnp.concatenate([rows[3 * ((place[2] + SHIFT[s]) % H) + j] for s in range(H)], axis=0)
            for j in range(3)
        ],
        axis=1,
    )
    right = jnp.concatenate([c[which] for c in (c0, c1, c2, c3)], axis=1)
    found = lax.dot_general(
        left, right, (((0,), (0,)), ((), ())), preferred_element_type=jnp.float32
    )
    for i in range(X):
        out[i] = found[:, i * WIDTH : (i + 1) * WIDTH].astype(out.dtype)


SMEM = pl.BlockSpec(memory_space=pltpu.SMEM)
VMEM = pl.BlockSpec(memory_space=pltpu.VMEM)


def product(side, place, rows, columns, dtype):
    return pl.pallas_call(
        functools.partial(product_kernel, side),
        out_shape=jax.ShapeDtypeStruct((X, 3 * WIDTH, WIDTH), dtype),
        in_specs=[SMEM] + [VMEM] * (1 + X),
        out_specs=VMEM,
        compiler_params=pltpu.CompilerParams(vmem_limit_bytes=16 * 2**20),
        cost_estimate=pl.CostEstimate(flops=4 * 10**8, bytes_accessed=3 * 10**6, transcendentals=0),
    )(place, rows, *columns)


def total_kernel(place, keep, taken, *outs):
    for r, out in enumerate(outs):
        i = (r + place[3]) % X
        out[...] = (keep[i] + taken[i].astype(jnp.float32)).astype(out.dtype)


def add_partner(place, keep, taken):
    return pl.pallas_call(
        total_kernel,
        out_shape=[jax.ShapeDtypeStruct(keep.shape[1:], jnp.bfloat16)] * X,
        in_specs=[SMEM, VMEM, VMEM],
        out_specs=[VMEM] * X,
        compiler_params=pltpu.CompilerParams(vmem_limit_bytes=8 * 2**20),
        name="total",
    )(place, keep, taken)


def assemble_kernel(place, f0, f1, f2, f3, out):
    for i, piece in enumerate((f0, f1, f2, f3)):
        t = place[4 + i]
        for j in range(3):
            out[t % 2, j, t // 2] = piece[j * WIDTH : (j + 1) * WIDTH, :].astype(jnp.float32)


def assemble(place, pieces):
    return pl.pallas_call(
        assemble_kernel,
        out_shape=jax.ShapeDtypeStruct((2, 3, 2, WIDTH, WIDTH), jnp.float32),
        in_specs=[SMEM] + [VMEM] * 4,
        out_specs=VMEM,
        compiler_params=pltpu.CompilerParams(vmem_limit_bytes=8 * 2**20),
        name="assemble",
    )(place, *pieces)


def blocks(pair_matrix, band_energy, occupation, pair_first, pair_second, pair_kpoint):
    pool, col = lax.axis_index("pool"), lax.axis_index("col")
    k, x, l = pool % K, col // (Z * L), col % L
    place = jnp.stack(
        [1 - k, k, x, 2 * l] + [(x - 2 * k - r) % X for r in range(X)]
    ).astype(jnp.int32)

    around = []
    for s in range(1, H):
        around.append(move(pair_matrix, lambda h, k, x, z, l, s=s: (h - s, k, x, z, l)))
    scaled = scaled_block(
        band_energy, occupation, pair_first, pair_second, pair_kpoint, pair_matrix
    )
    sent = move(
        scaled,
        lambda h, k, x, z, l: (x, k, z // 3, z + 3 * SHIFT[(h - x) % H], l),
    )
    own = jnp.concatenate([pair_matrix] + around, axis=0)
    other = move(own, lambda h, k, x, z, l: (h, k, x, z, 1 - l))
    both = jnp.stack([own, other])
    columns = [both]
    for s in range(1, X):
        columns.append(move(both, lambda h, k, x, z, l, s=s: (h, k, x - s, z, l)))
    rows = lax.all_gather(sent, "col", axis=0, axis_index_groups=Z_GROUPS)

    give = product(0, place, rows, columns, jnp.bfloat16)
    taken = move(give, lambda h, k, x, z, l: (h, 1 - k, x, z, l))
    keep = product(1, place, rows, columns, jnp.float32)
    total = add_partner(place, keep, taken)
    home = []
    for r in range(X):
        home.append(
            move(
                total[r],
                lambda h, k, x, z, l, r=r: (h, x // 2, x + r + 2 * l, z, l ^ k),
            )
        )
    return assemble(place, home).reshape(-1, WIDTH)


def solution(mesh):
    return jax.shard_map(
        blocks,
        mesh=mesh,
        in_specs=(
            P("pool", "col"),
            P("pool", None, None),
            P("pool", None, None),
            P("pool", None),
            P("pool", None),
            P("pool", None),
        ),
        out_specs=P("pool", "col"),
        check_vma=False,
    )
```

```python
import functools

import jax
import jax.numpy as jnp
from jax import lax
from jax.experimental import pallas as pl
from jax.experimental.pallas import tpu as pltpu
from jax.sharding import PartitionSpec as P


H, K, X, Z, L = 4, 2, 4, 12, 2
COLS = X * Z * L
PAIRS, WIDTH = 256, 128
AXES = ("pool", "col")
NEAR = ((9, 5, 8), (11, 1, 6), (0, 2, 4), (10, 3, 7))


def at(h, k, x, z, l):
    return ((h % H) * K + k) * COLS + (x % X) * (Z * L) + (z % Z) * L + l


def table(f):
    return [
        (at(h, k, x, z, l), at(*f(h, k, x, z, l)))
        for h in range(H)
        for k in range(K)
        for x in range(X)
        for z in range(Z)
        for l in range(L)
    ]


def move(value, f):
    return lax.ppermute(value, AXES, table(f))


def spread(h, k, x, z, l):
    side, (j, a) = z // 6, divmod(z % 6, 2)
    return x, k, 2 * side + a, NEAR[(h - x) % H][j] + 6 * side + a, l


H_GROUPS = [[h * K + k for h in range(H)] for k in range(K)]
Z_GROUPS = [[x * Z * L + z * L + l for z in range(Z)] for x in range(X) for l in range(L)]


def scale_kernel(energy, occupied, first, second, kpoint, block, out, energies, filled):
    chunks = energy.shape[-1] // WIDTH
    kpts = energy.shape[-2]
    for c in range(chunks):
        part = pl.ds(c * WIDTH, WIDTH)
        energies[pl.ds(c * kpts, kpts), :] = energy[0, :, part]
        filled[pl.ds(c * kpts, kpts), :] = occupied[0, :, part].astype(jnp.float32)

    def pick(table_ref, band):
        entries = table_ref.shape[0]
        place = (band // WIDTH) * kpts + kpoint[...]
        spot = band % WIDTH
        pairs = band.shape[-1]
        one = (lax.broadcasted_iota(jnp.int32, (entries, pairs), 0) == place).astype(jnp.float32)
        found = lax.dot_general(
            table_ref[...],
            one,
            (((0,), (0,)), ((), ())),
            precision=lax.Precision.HIGHEST,
            preferred_element_type=jnp.float32,
        )
        keep = lax.broadcasted_iota(jnp.int32, (WIDTH, pairs), 0) == spot
        return jnp.sum(jnp.where(keep, found, 0.0), axis=0, keepdims=True)

    a, b = first[...], second[...]
    gap = jnp.abs(pick(energies, b) - pick(energies, a))
    change = pick(filled, a) - pick(filled, b)
    weight = 2.0 * change / (1.0 + gap)
    for i in range(PAIRS // WIDTH):
        rows = pl.ds(i * WIDTH, WIDTH)
        factor = jnp.broadcast_to(weight[:, i * WIDTH : (i + 1) * WIDTH], (WIDTH, WIDTH)).T
        out[rows, :] = (block[rows, :].astype(jnp.float32) * factor).astype(jnp.bfloat16)


def scaled_block(energy, occupied, first, second, kpoint, block):
    entries = energy.shape[1] * energy.shape[2] // WIDTH
    return pl.pallas_call(
        scale_kernel,
        out_shape=jax.ShapeDtypeStruct(block.shape, jnp.bfloat16),
        scratch_shapes=[pltpu.VMEM((entries, WIDTH), jnp.float32)] * 2,
        cost_estimate=pl.CostEstimate(flops=4 * 10**8, bytes_accessed=3 * 10**5, transcendentals=0),
        name="scale",
    )(energy, occupied, first, second, kpoint, block)


def product_kernel(side, place, rows, c0, c1, c2, c3, out):
    which = place[side]

    def columns(c, s):
        start = pl.multiple_of(((place[8] + s) % H) * PAIRS, PAIRS)
        return c[which, pl.ds(start, PAIRS), :]

    left = jnp.concatenate(
        [
            jnp.concatenate([rows[(NEAR[s][j] + place[2]) % Z] for s in range(H)], axis=0)
            for j in range(3)
        ],
        axis=1,
    )
    right = jnp.concatenate(
        [
            jnp.concatenate([columns(c, s) for s in range(H)], axis=0)
            for c in (c0, c1, c2, c3)
        ],
        axis=1,
    )
    found = lax.dot_general(
        left, right, (((0,), (0,)), ((), ())), preferred_element_type=jnp.float32
    )
    for i in range(X):
        out[i] = found[:, i * WIDTH : (i + 1) * WIDTH].astype(out.dtype)


SMEM = pl.BlockSpec(memory_space=pltpu.SMEM)
VMEM = pl.BlockSpec(memory_space=pltpu.VMEM)


def product(side, place, rows, columns, dtype):
    return pl.pallas_call(
        functools.partial(product_kernel, side),
        out_shape=jax.ShapeDtypeStruct((X, 3 * WIDTH, WIDTH), dtype),
        in_specs=[SMEM] + [VMEM] * (1 + X),
        out_specs=VMEM,
        compiler_params=pltpu.CompilerParams(vmem_limit_bytes=16 * 2**20),
        cost_estimate=pl.CostEstimate(flops=4 * 10**8, bytes_accessed=3 * 10**6, transcendentals=0),
    )(place, rows, *columns)


def total_kernel(place, keep, taken, *outs):
    for r, out in enumerate(outs):
        i = (r + place[3]) % X
        out[...] = (keep[i] + taken[i].astype(jnp.float32)).astype(out.dtype)


def add_partner(place, keep, taken):
    return pl.pallas_call(
        total_kernel,
        out_shape=[jax.ShapeDtypeStruct(keep.shape[1:], jnp.bfloat16)] * X,
        in_specs=[SMEM, VMEM, VMEM],
        out_specs=[VMEM] * X,
        compiler_params=pltpu.CompilerParams(vmem_limit_bytes=8 * 2**20),
        name="total",
    )(place, keep, taken)


def assemble_kernel(place, f0, f1, f2, f3, out):
    for i, piece in enumerate((f0, f1, f2, f3)):
        t = place[4 + i]
        for j in range(3):
            out[j, t % 2, t // 2] = piece[j * WIDTH : (j + 1) * WIDTH, :].astype(jnp.float32)


def assemble(place, pieces):
    return pl.pallas_call(
        assemble_kernel,
        out_shape=jax.ShapeDtypeStruct((3, 2, 2, WIDTH, WIDTH), jnp.float32),
        in_specs=[SMEM] + [VMEM] * 4,
        out_specs=VMEM,
        compiler_params=pltpu.CompilerParams(vmem_limit_bytes=8 * 2**20),
        name="assemble",
    )(place, *pieces)


def blocks(pair_matrix, band_energy, occupation, pair_first, pair_second, pair_kpoint):
    pool, col = lax.axis_index("pool"), lax.axis_index("col")
    k, x, l = pool % K, col // (Z * L), col % L
    place = jnp.stack(
        [1 - k, k, 6 * (x // 2) + x % 2, 2 * l]
        + [(x - 2 * k - r) % X for r in range(X)]
        + [pool // K]
    ).astype(jnp.int32)

    own = lax.all_gather(
        pair_matrix, "pool", axis=0, tiled=True, axis_index_groups=H_GROUPS
    )
    scaled = scaled_block(
        band_energy, occupation, pair_first, pair_second, pair_kpoint, pair_matrix
    )
    sent = move(scaled, spread)
    other = move(own, lambda h, k, x, z, l: (h, k, x, z, 1 - l))
    both = jnp.stack([own, other])
    columns = [both]
    for s in range(1, X):
        columns.append(move(both, lambda h, k, x, z, l, s=s: (h, k, x - s, z, l)))
    rows = lax.all_gather(sent, "col", axis=0, axis_index_groups=Z_GROUPS)

    give = product(0, place, rows, columns, jnp.bfloat16)
    taken = move(give, lambda h, k, x, z, l: (h, 1 - k, x, z, l))
    keep = product(1, place, rows, columns, jnp.float32)
    total = add_partner(place, keep, taken)
    home = []
    for r in range(X):
        home.append(
            move(
                total[r],
                lambda h, k, x, z, l, r=r: (h, x // 2, x + r + 2 * l, z, l ^ k),
            )
        )
    return assemble(place, home).reshape(-1, WIDTH)


def solution(mesh):
    return jax.shard_map(
        blocks,
        mesh=mesh,
        in_specs=(
            P("pool", "col"),
            P("pool", None, None),
            P("pool", None, None),
            P("pool", None),
            P("pool", None),
            P("pool", None),
        ),
        out_specs=P("pool", "col"),
        check_vma=False,
    )
```

```python
import functools

import jax
import jax.numpy as jnp
from jax import lax
from jax.experimental import pallas as pl
from jax.experimental.pallas import tpu as pltpu
from jax.sharding import PartitionSpec as P


H, K, X, Z, L = 4, 2, 4, 12, 2
COLS = X * Z * L
PAIRS, WIDTH = 256, 128
AXES = ("pool", "col")
NEAR = ((9, 5, 8), (11, 1, 6), (0, 2, 4), (10, 3, 7))


def at(h, k, x, z, l):
    return ((h % H) * K + k) * COLS + (x % X) * (Z * L) + (z % Z) * L + l


def table(f):
    return [
        (at(h, k, x, z, l), at(*f(h, k, x, z, l)))
        for h in range(H)
        for k in range(K)
        for x in range(X)
        for z in range(Z)
        for l in range(L)
    ]


def move(value, f):
    return lax.ppermute(value, AXES, table(f))


def spread(h, k, x, z, l):
    side, (j, a) = z // 6, divmod(z % 6, 2)
    return x, k, 2 * side + a, NEAR[(h - x) % H][j] + 6 * side + a, l


Z_GROUPS = [[x * Z * L + z * L + l for z in range(Z)] for x in range(X) for l in range(L)]


def scale_kernel(energy, occupied, first, second, kpoint, block, out, energies, filled):
    chunks = energy.shape[-1] // WIDTH
    kpts = energy.shape[-2]
    for c in range(chunks):
        part = pl.ds(c * WIDTH, WIDTH)
        energies[pl.ds(c * kpts, kpts), :] = energy[0, :, part]
        filled[pl.ds(c * kpts, kpts), :] = occupied[0, :, part].astype(jnp.float32)

    def pick(table_ref, band):
        entries = table_ref.shape[0]
        place = (band // WIDTH) * kpts + kpoint[...]
        spot = band % WIDTH
        pairs = band.shape[-1]
        one = (lax.broadcasted_iota(jnp.int32, (entries, pairs), 0) == place).astype(jnp.float32)
        found = lax.dot_general(
            table_ref[...],
            one,
            (((0,), (0,)), ((), ())),
            precision=lax.Precision.HIGHEST,
            preferred_element_type=jnp.float32,
        )
        keep = lax.broadcasted_iota(jnp.int32, (WIDTH, pairs), 0) == spot
        return jnp.sum(jnp.where(keep, found, 0.0), axis=0, keepdims=True)

    a, b = first[...], second[...]
    gap = jnp.abs(pick(energies, b) - pick(energies, a))
    change = pick(filled, a) - pick(filled, b)
    weight = 2.0 * change / (1.0 + gap)
    for i in range(PAIRS // WIDTH):
        rows = pl.ds(i * WIDTH, WIDTH)
        factor = jnp.broadcast_to(weight[:, i * WIDTH : (i + 1) * WIDTH], (WIDTH, WIDTH)).T
        out[rows, :] = (block[rows, :].astype(jnp.float32) * factor).astype(jnp.bfloat16)


def scaled_block(energy, occupied, first, second, kpoint, block):
    entries = energy.shape[1] * energy.shape[2] // WIDTH
    return pl.pallas_call(
        scale_kernel,
        out_shape=jax.ShapeDtypeStruct(block.shape, jnp.bfloat16),
        scratch_shapes=[pltpu.VMEM((entries, WIDTH), jnp.float32)] * 2,
        cost_estimate=pl.CostEstimate(flops=4 * 10**8, bytes_accessed=3 * 10**5, transcendentals=0),
        name="scale",
    )(energy, occupied, first, second, kpoint, block)


def product_kernel(side, place, rows, c0, c1, c2, c3, out):
    which = place[side]
    left = jnp.concatenate(
        [
            jnp.concatenate([rows[(NEAR[s][j] + place[2]) % Z] for s in range(H)], axis=0)
            for j in range(3)
        ],
        axis=1,
    )
    right = jnp.concatenate([c[which] for c in (c0, c1, c2, c3)], axis=1)
    found = lax.dot_general(
        left, right, (((0,), (0,)), ((), ())), preferred_element_type=jnp.float32
    )
    for i in range(X):
        out[i] = found[:, i * WIDTH : (i + 1) * WIDTH].astype(out.dtype)


SMEM = pl.BlockSpec(memory_space=pltpu.SMEM)
VMEM = pl.BlockSpec(memory_space=pltpu.VMEM)


def product(side, place, rows, columns, dtype):
    return pl.pallas_call(
        functools.partial(product_kernel, side),
        out_shape=jax.ShapeDtypeStruct((X, 3 * WIDTH, WIDTH), dtype),
        in_specs=[SMEM] + [VMEM] * (1 + X),
        out_specs=VMEM,
        compiler_params=pltpu.CompilerParams(vmem_limit_bytes=16 * 2**20),
        cost_estimate=pl.CostEstimate(flops=4 * 10**8, bytes_accessed=3 * 10**6, transcendentals=0),
    )(place, rows, *columns)


def total_kernel(place, keep, taken, *outs):
    for r, out in enumerate(outs):
        i = (r + place[3]) % X
        out[...] = (keep[i] + taken[i].astype(jnp.float32)).astype(out.dtype)


def add_partner(place, keep, taken):
    return pl.pallas_call(
        total_kernel,
        out_shape=[jax.ShapeDtypeStruct(keep.shape[1:], jnp.bfloat16)] * X,
        in_specs=[SMEM, VMEM, VMEM],
        out_specs=[VMEM] * X,
        compiler_params=pltpu.CompilerParams(vmem_limit_bytes=8 * 2**20),
        name="total",
    )(place, keep, taken)


def settle_kernel(start, count, place, *refs):
    pieces, (out, wide, sems) = refs[:count], refs[-3:]
    copies = []
    for i, piece in enumerate(pieces):
        t = place[4 + start + i]
        for j in range(3):
            wide[i, j] = piece[j * WIDTH : (j + 1) * WIDTH, :].astype(jnp.float32)
            copies.append(
                pltpu.make_async_copy(wide.at[i, j], out.at[j, t % 2, t // 2], sems.at[i, j])
            )
            copies[-1].start()
    for copy in copies:
        copy.wait()


def settle(place, start, pieces, out=None):
    count = len(pieces)
    given = [] if out is None else [out]
    return pl.pallas_call(
        functools.partial(settle_kernel, start, count),
        out_shape=jax.ShapeDtypeStruct((3, 2, 2, WIDTH, WIDTH), jnp.float32),
        in_specs=[SMEM] + [VMEM] * count + [pl.BlockSpec(memory_space=pl.ANY)] * len(given),
        out_specs=pl.BlockSpec(memory_space=pl.ANY),
        scratch_shapes=[
            pltpu.VMEM((count, 3, WIDTH, WIDTH), jnp.float32),
            pltpu.SemaphoreType.DMA((count, 3)),
        ],
        input_output_aliases={1 + count: 0} if given else {},
        compiler_params=pltpu.CompilerParams(vmem_limit_bytes=8 * 2**20),
    )(place, *pieces, *given)


def blocks(pair_matrix, band_energy, occupation, pair_first, pair_second, pair_kpoint):
    pool, col = lax.axis_index("pool"), lax.axis_index("col")
    k, x, l = pool % K, col // (Z * L), col % L
    place = jnp.stack(
        [1 - k, k, 6 * (x // 2) + x % 2, 2 * l]
        + [(x - 2 * k - r) % X for r in range(X)]
    ).astype(jnp.int32)

    around = []
    for s in range(1, H):
        around.append(move(pair_matrix, lambda h, k, x, z, l, s=s: (h - s, k, x, z, l)))
    scaled = scaled_block(
        band_energy, occupation, pair_first, pair_second, pair_kpoint, pair_matrix
    )
    sent = move(scaled, spread)
    own = jnp.concatenate([pair_matrix] + around, axis=0)
    other = move(own, lambda h, k, x, z, l: (h, k, x, z, 1 - l))
    both = jnp.stack([own, other])
    columns = [both]
    for s in range(1, X):
        columns.append(move(both, lambda h, k, x, z, l, s=s: (h, k, x - s, z, l)))
    rows = lax.all_gather(sent, "col", axis=0, axis_index_groups=Z_GROUPS)

    give = product(0, place, rows, columns, jnp.bfloat16)
    taken = move(give, lambda h, k, x, z, l: (h, 1 - k, x, z, l))
    keep = product(1, place, rows, columns, jnp.float32)
    total = add_partner(place, keep, taken)
    home = []
    for r in range(X):
        home.append(
            move(
                total[r],
                lambda h, k, x, z, l, r=r: (h, x // 2, x + r + 2 * l, z, l ^ k),
            )
        )
    most = settle(place, 0, home[:3])
    return settle(place, 3, home[3:], most).reshape(-1, WIDTH)


def solution(mesh):
    return jax.shard_map(
        blocks,
        mesh=mesh,
        in_specs=(
            P("pool", "col"),
            P("pool", None, None),
            P("pool", None, None),
            P("pool", None),
            P("pool", None),
            P("pool", None),
        ),
        out_specs=P("pool", "col"),
        check_vma=False,
    )
```

```python
import functools

import jax
import jax.numpy as jnp
from jax import lax
from jax.experimental import pallas as pl
from jax.experimental.pallas import tpu as pltpu
from jax.sharding import PartitionSpec as P


H, K, X, Z, L = 4, 2, 4, 12, 2
COLS = X * Z * L
PAIRS, WIDTH = 256, 128
AXES = ("pool", "col")
NEAR = ((9, 5, 8), (11, 1, 6), (0, 2, 4), (10, 3, 7))


def at(h, k, x, z, l):
    return ((h % H) * K + k) * COLS + (x % X) * (Z * L) + (z % Z) * L + l


def table(f):
    return [
        (at(h, k, x, z, l), at(*f(h, k, x, z, l)))
        for h in range(H)
        for k in range(K)
        for x in range(X)
        for z in range(Z)
        for l in range(L)
    ]


def move(value, f):
    return lax.ppermute(value, AXES, table(f))


def spread(h, k, x, z, l):
    side, (j, a) = z // 6, divmod(z % 6, 2)
    return x, k, 2 * side + a, NEAR[(h - x) % H][j] + 6 * side + a, l


Y_GROUPS = [
    [at(h, k, x, z, l) for h in range(H) for l in range(L)]
    for k in range(K)
    for x in range(X)
    for z in range(Z)
]
Z_GROUPS = [[x * Z * L + z * L + l for z in range(Z)] for x in range(X) for l in range(L)]


def scale_kernel(energy, occupied, first, second, kpoint, block, out, energies, filled):
    chunks = energy.shape[-1] // WIDTH
    kpts = energy.shape[-2]
    for c in range(chunks):
        part = pl.ds(c * WIDTH, WIDTH)
        energies[pl.ds(c * kpts, kpts), :] = energy[0, :, part]
        filled[pl.ds(c * kpts, kpts), :] = occupied[0, :, part].astype(jnp.float32)

    def pick(table_ref, band):
        entries = table_ref.shape[0]
        place = (band // WIDTH) * kpts + kpoint[...]
        spot = band % WIDTH
        pairs = band.shape[-1]
        one = (lax.broadcasted_iota(jnp.int32, (entries, pairs), 0) == place).astype(jnp.float32)
        found = lax.dot_general(
            table_ref[...],
            one,
            (((0,), (0,)), ((), ())),
            precision=lax.Precision.HIGHEST,
            preferred_element_type=jnp.float32,
        )
        keep = lax.broadcasted_iota(jnp.int32, (WIDTH, pairs), 0) == spot
        return jnp.sum(jnp.where(keep, found, 0.0), axis=0, keepdims=True)

    a, b = first[...], second[...]
    gap = jnp.abs(pick(energies, b) - pick(energies, a))
    change = pick(filled, a) - pick(filled, b)
    weight = 2.0 * change / (1.0 + gap)
    for i in range(PAIRS // WIDTH):
        rows = pl.ds(i * WIDTH, WIDTH)
        factor = jnp.broadcast_to(weight[:, i * WIDTH : (i + 1) * WIDTH], (WIDTH, WIDTH)).T
        out[rows, :] = (block[rows, :].astype(jnp.float32) * factor).astype(jnp.bfloat16)


def scaled_block(energy, occupied, first, second, kpoint, block):
    entries = energy.shape[1] * energy.shape[2] // WIDTH
    return pl.pallas_call(
        scale_kernel,
        out_shape=jax.ShapeDtypeStruct(block.shape, jnp.bfloat16),
        scratch_shapes=[pltpu.VMEM((entries, WIDTH), jnp.float32)] * 2,
        cost_estimate=pl.CostEstimate(flops=4 * 10**8, bytes_accessed=3 * 10**5, transcendentals=0),
        name="scale",
    )(energy, occupied, first, second, kpoint, block)


def product_kernel(side, place, rows, c0, c1, c2, c3, out):
    which = place[side]

    def columns(c, s):
        return c[((place[8] + s) % H) * L + which]

    left = jnp.concatenate(
        [
            jnp.concatenate([rows[(NEAR[s][j] + place[2]) % Z] for s in range(H)], axis=0)
            for j in range(3)
        ],
        axis=1,
    )
    right = jnp.concatenate(
        [
            jnp.concatenate([columns(c, s) for s in range(H)], axis=0)
            for c in (c0, c1, c2, c3)
        ],
        axis=1,
    )
    found = lax.dot_general(
        left, right, (((0,), (0,)), ((), ())), preferred_element_type=jnp.float32
    )
    for i in range(X):
        out[i] = found[:, i * WIDTH : (i + 1) * WIDTH].astype(out.dtype)


SMEM = pl.BlockSpec(memory_space=pltpu.SMEM)
VMEM = pl.BlockSpec(memory_space=pltpu.VMEM)


def product(side, place, rows, columns, dtype):
    return pl.pallas_call(
        functools.partial(product_kernel, side),
        out_shape=jax.ShapeDtypeStruct((X, 3 * WIDTH, WIDTH), dtype),
        in_specs=[SMEM] + [VMEM] * (1 + X),
        out_specs=VMEM,
        compiler_params=pltpu.CompilerParams(vmem_limit_bytes=16 * 2**20),
        cost_estimate=pl.CostEstimate(flops=4 * 10**8, bytes_accessed=3 * 10**6, transcendentals=0),
    )(place, rows, *columns)


def total_kernel(place, keep, taken, *outs):
    for r, out in enumerate(outs):
        i = (r + place[3]) % X
        out[...] = (keep[i] + taken[i].astype(jnp.float32)).astype(out.dtype)


def add_partner(place, keep, taken):
    return pl.pallas_call(
        total_kernel,
        out_shape=[jax.ShapeDtypeStruct(keep.shape[1:], jnp.bfloat16)] * X,
        in_specs=[SMEM, VMEM, VMEM],
        out_specs=[VMEM] * X,
        compiler_params=pltpu.CompilerParams(vmem_limit_bytes=8 * 2**20),
        name="total",
    )(place, keep, taken)


def assemble_kernel(place, f0, f1, f2, f3, out):
    for i, piece in enumerate((f0, f1, f2, f3)):
        t = place[4 + i]
        for j in range(3):
            out[j, t % 2, t // 2] = piece[j * WIDTH : (j + 1) * WIDTH, :].astype(jnp.float32)


def assemble(place, pieces):
    return pl.pallas_call(
        assemble_kernel,
        out_shape=jax.ShapeDtypeStruct((3, 2, 2, WIDTH, WIDTH), jnp.float32),
        in_specs=[SMEM] + [VMEM] * 4,
        out_specs=VMEM,
        compiler_params=pltpu.CompilerParams(vmem_limit_bytes=8 * 2**20),
        name="assemble",
    )(place, *pieces)


def blocks(pair_matrix, band_energy, occupation, pair_first, pair_second, pair_kpoint):
    pool, col = lax.axis_index("pool"), lax.axis_index("col")
    k, x, l = pool % K, col // (Z * L), col % L
    place = jnp.stack(
        [(l + 1 - k) % L, (l + k) % L, 6 * (x // 2) + x % 2, 2 * l]
        + [(x - 2 * k - r) % X for r in range(X)]
        + [pool // K]
    ).astype(jnp.int32)

    sent = move(pair_matrix, spread)
    scaled = scaled_block(
        band_energy, occupation, pair_first, pair_second, pair_kpoint, pair_matrix
    )
    both = lax.all_gather(scaled, AXES, axis=0, axis_index_groups=Y_GROUPS)
    columns = [both]
    for s in range(1, X):
        columns.append(move(both, lambda h, k, x, z, l, s=s: (h, k, x - s, z, l)))
    rows = lax.all_gather(sent, "col", axis=0, axis_index_groups=Z_GROUPS)

    give = product(0, place, rows, columns, jnp.bfloat16)
    taken = move(give, lambda h, k, x, z, l: (h, 1 - k, x, z, l))
    keep = product(1, place, rows, columns, jnp.float32)
    total = add_partner(place, keep, taken)
    home = []
    for r in range(X):
        home.append(
            move(
                total[r],
                lambda h, k, x, z, l, r=r: (h, x // 2, x + r + 2 * l, z, l ^ k),
            )
        )
    return assemble(place, home).reshape(-1, WIDTH)


def solution(mesh):
    return jax.shard_map(
        blocks,
        mesh=mesh,
        in_specs=(
            P("pool", "col"),
            P("pool", None, None),
            P("pool", None, None),
            P("pool", None),
            P("pool", None),
            P("pool", None),
        ),
        out_specs=P("pool", "col"),
        check_vma=False,
    )
```

```python
import functools

import jax
import jax.numpy as jnp
from jax import lax
from jax.experimental import pallas as pl
from jax.experimental.pallas import tpu as pltpu
from jax.sharding import PartitionSpec as P


H, K, X, Z, L = 4, 2, 4, 12, 2
COLS = X * Z * L
PAIRS, WIDTH = 256, 128
AXES = ("pool", "col")
NEAR = ((9, 5, 8), (11, 1, 6), (0, 2, 4), (10, 3, 7))


def at(h, k, x, z, l):
    return ((h % H) * K + k) * COLS + (x % X) * (Z * L) + (z % Z) * L + l


def table(f):
    return [
        (at(h, k, x, z, l), at(*f(h, k, x, z, l)))
        for h in range(H)
        for k in range(K)
        for x in range(X)
        for z in range(Z)
        for l in range(L)
    ]


def move(value, f):
    return lax.ppermute(value, AXES, table(f))


def spread(h, k, x, z, l):
    side, (j, a) = z // 6, divmod(z % 6, 2)
    return x, k, 2 * side + a, NEAR[(h - x) % H][j] + 6 * side + a, l


H_GROUPS = [[h * K + k for h in range(H)] for k in range(K)]
Z_GROUPS = [[x * Z * L + z * L + l for z in range(Z)] for x in range(X) for l in range(L)]


def scale_kernel(energy, occupied, first, second, kpoint, own, other, out, energies, filled):
    chunks = energy.shape[-1] // WIDTH
    kpts = energy.shape[-2]
    for c in range(chunks):
        part = pl.ds(c * WIDTH, WIDTH)
        energies[pl.ds(c * kpts, kpts), :] = energy[0, :, part]
        filled[pl.ds(c * kpts, kpts), :] = occupied[0, :, part].astype(jnp.float32)

    def pick(table_ref, band):
        entries = table_ref.shape[0]
        place = (band // WIDTH) * kpts + kpoint[...]
        spot = band % WIDTH
        pairs = band.shape[-1]
        one = (lax.broadcasted_iota(jnp.int32, (entries, pairs), 0) == place).astype(jnp.float32)
        found = lax.dot_general(
            table_ref[...],
            one,
            (((0,), (0,)), ((), ())),
            precision=lax.Precision.HIGHEST,
            preferred_element_type=jnp.float32,
        )
        keep = lax.broadcasted_iota(jnp.int32, (WIDTH, pairs), 0) == spot
        return jnp.sum(jnp.where(keep, found, 0.0), axis=0, keepdims=True)

    a, b = first[...], second[...]
    gap = jnp.abs(pick(energies, b) - pick(energies, a))
    change = pick(filled, a) - pick(filled, b)
    weight = 2.0 * change / (1.0 + gap)
    for i in range(PAIRS // WIDTH):
        rows = pl.ds(i * WIDTH, WIDTH)
        factor = jnp.broadcast_to(weight[:, i * WIDTH : (i + 1) * WIDTH], (WIDTH, WIDTH)).T
        for n, block in enumerate((own, other)):
            out[n, rows, :] = (block[rows, :].astype(jnp.float32) * factor).astype(jnp.bfloat16)


def scaled_blocks(energy, occupied, first, second, kpoint, own, other):
    entries = energy.shape[1] * energy.shape[2] // WIDTH
    return pl.pallas_call(
        scale_kernel,
        out_shape=jax.ShapeDtypeStruct((2,) + own.shape, jnp.bfloat16),
        scratch_shapes=[pltpu.VMEM((entries, WIDTH), jnp.float32)] * 2,
        compiler_params=pltpu.CompilerParams(vmem_limit_bytes=8 * 2**20),
        cost_estimate=pl.CostEstimate(flops=4 * 10**8, bytes_accessed=3 * 10**5, transcendentals=0),
        name="scale",
    )(energy, occupied, first, second, kpoint, own, other)


def product_kernel(side, place, rows, c0, c1, c2, c3, out):
    which = place[side]

    def columns(c, s):
        return c[((place[8] + s) % H) * L + which]

    left = jnp.concatenate(
        [
            jnp.concatenate([rows[(NEAR[s][j] + place[2]) % Z] for s in range(H)], axis=0)
            for j in range(3)
        ],
        axis=1,
    )
    right = jnp.concatenate(
        [
            jnp.concatenate([columns(c, s) for s in range(H)], axis=0)
            for c in (c0, c1, c2, c3)
        ],
        axis=1,
    )
    found = lax.dot_general(
        left, right, (((0,), (0,)), ((), ())), preferred_element_type=jnp.float32
    )
    for i in range(X):
        out[i] = found[:, i * WIDTH : (i + 1) * WIDTH].astype(out.dtype)


SMEM = pl.BlockSpec(memory_space=pltpu.SMEM)
VMEM = pl.BlockSpec(memory_space=pltpu.VMEM)


def product(side, place, rows, columns, dtype):
    return pl.pallas_call(
        functools.partial(product_kernel, side),
        out_shape=jax.ShapeDtypeStruct((X, 3 * WIDTH, WIDTH), dtype),
        in_specs=[SMEM] + [VMEM] * (1 + X),
        out_specs=VMEM,
        compiler_params=pltpu.CompilerParams(vmem_limit_bytes=16 * 2**20),
        cost_estimate=pl.CostEstimate(flops=4 * 10**8, bytes_accessed=3 * 10**6, transcendentals=0),
    )(place, rows, *columns)


def total_kernel(place, keep, taken, *outs):
    for r, out in enumerate(outs):
        i = (r + place[3]) % X
        out[...] = (keep[i] + taken[i].astype(jnp.float32)).astype(out.dtype)


def add_partner(place, keep, taken):
    return pl.pallas_call(
        total_kernel,
        out_shape=[jax.ShapeDtypeStruct(keep.shape[1:], jnp.bfloat16)] * X,
        in_specs=[SMEM, VMEM, VMEM],
        out_specs=[VMEM] * X,
        compiler_params=pltpu.CompilerParams(vmem_limit_bytes=8 * 2**20),
        name="total",
    )(place, keep, taken)


def assemble_kernel(place, f0, f1, f2, f3, out):
    for i, piece in enumerate((f0, f1, f2, f3)):
        t = place[4 + i]
        for j in range(3):
            out[j, t % 2, t // 2] = piece[j * WIDTH : (j + 1) * WIDTH, :].astype(jnp.float32)


def assemble(place, pieces):
    return pl.pallas_call(
        assemble_kernel,
        out_shape=jax.ShapeDtypeStruct((3, 2, 2, WIDTH, WIDTH), jnp.float32),
        in_specs=[SMEM] + [VMEM] * 4,
        out_specs=VMEM,
        compiler_params=pltpu.CompilerParams(vmem_limit_bytes=8 * 2**20),
        name="assemble",
    )(place, *pieces)


def blocks(pair_matrix, band_energy, occupation, pair_first, pair_second, pair_kpoint):
    pool, col = lax.axis_index("pool"), lax.axis_index("col")
    k, x, l = pool % K, col // (Z * L), col % L
    place = jnp.stack(
        [1 - k, k, 6 * (x // 2) + x % 2, 2 * l]
        + [(x - 2 * k - r) % X for r in range(X)]
        + [pool // K]
    ).astype(jnp.int32)

    other = move(pair_matrix, lambda h, k, x, z, l: (h, k, x, z, 1 - l))
    sent = move(pair_matrix, spread)
    scaled = scaled_blocks(
        band_energy, occupation, pair_first, pair_second, pair_kpoint, pair_matrix, other
    )
    both = lax.all_gather(scaled, "pool", axis=0, tiled=True, axis_index_groups=H_GROUPS)
    columns = [both]
    for s in range(1, X):
        columns.append(move(both, lambda h, k, x, z, l, s=s: (h, k, x - s, z, l)))
    rows = lax.all_gather(sent, "col", axis=0, axis_index_groups=Z_GROUPS)

    give = product(0, place, rows, columns, jnp.bfloat16)
    taken = move(give, lambda h, k, x, z, l: (h, 1 - k, x, z, l))
    keep = product(1, place, rows, columns, jnp.float32)
    total = add_partner(place, keep, taken)
    home = []
    for r in range(X):
        home.append(
            move(
                total[r],
                lambda h, k, x, z, l, r=r: (h, x // 2, x + r + 2 * l, z, l ^ k),
            )
        )
    return assemble(place, home).reshape(-1, WIDTH)


def solution(mesh):
    return jax.shard_map(
        blocks,
        mesh=mesh,
        in_specs=(
            P("pool", "col"),
            P("pool", None, None),
            P("pool", None, None),
            P("pool", None),
            P("pool", None),
            P("pool", None),
        ),
        out_specs=P("pool", "col"),
        check_vma=False,
    )
```

```python
import functools

import jax
import jax.numpy as jnp
from jax import lax
from jax.experimental import pallas as pl
from jax.experimental.pallas import tpu as pltpu
from jax.sharding import PartitionSpec as P


H, K, X, Z, L = 4, 2, 4, 12, 2
COLS = X * Z * L
PAIRS, WIDTH = 256, 128
AXES = ("pool", "col")
NEAR = ((9, 5, 8), (11, 1, 6), (0, 2, 4), (10, 3, 7))


def at(h, k, x, z, l):
    return ((h % H) * K + k) * COLS + (x % X) * (Z * L) + (z % Z) * L + l


def table(f):
    return [
        (at(h, k, x, z, l), at(*f(h, k, x, z, l)))
        for h in range(H)
        for k in range(K)
        for x in range(X)
        for z in range(Z)
        for l in range(L)
    ]


def move(value, f):
    return lax.ppermute(value, AXES, table(f))


def spread(h, k, x, z, l):
    side, (j, a) = z // 6, divmod(z % 6, 2)
    return x, k, 2 * side + a, NEAR[(h - x) % H][j] + 6 * side + a, l


Z_GROUPS = [[x * Z * L + z * L + l for z in range(Z)] for x in range(X) for l in range(L)]


def scale_kernel(energy, occupied, first, second, kpoint, own, other, out, energies, filled):
    chunks = energy.shape[-1] // WIDTH
    kpts = energy.shape[-2]
    for c in range(chunks):
        part = pl.ds(c * WIDTH, WIDTH)
        energies[pl.ds(c * kpts, kpts), :] = energy[0, :, part]
        filled[pl.ds(c * kpts, kpts), :] = occupied[0, :, part].astype(jnp.float32)

    def pick(table_ref, band):
        entries = table_ref.shape[0]
        place = (band // WIDTH) * kpts + kpoint[...]
        spot = band % WIDTH
        pairs = band.shape[-1]
        one = (lax.broadcasted_iota(jnp.int32, (entries, pairs), 0) == place).astype(jnp.float32)
        found = lax.dot_general(
            table_ref[...],
            one,
            (((0,), (0,)), ((), ())),
            precision=lax.Precision.HIGHEST,
            preferred_element_type=jnp.float32,
        )
        keep = lax.broadcasted_iota(jnp.int32, (WIDTH, pairs), 0) == spot
        return jnp.sum(jnp.where(keep, found, 0.0), axis=0, keepdims=True)

    a, b = first[...], second[...]
    gap = jnp.abs(pick(energies, b) - pick(energies, a))
    change = pick(filled, a) - pick(filled, b)
    weight = 2.0 * change / (1.0 + gap)
    for i in range(PAIRS // WIDTH):
        rows = pl.ds(i * WIDTH, WIDTH)
        factor = jnp.broadcast_to(weight[:, i * WIDTH : (i + 1) * WIDTH], (WIDTH, WIDTH)).T
        for n, block in enumerate((own, other)):
            out[n, rows, :] = (block[rows, :].astype(jnp.float32) * factor).astype(jnp.bfloat16)


def scaled_blocks(energy, occupied, first, second, kpoint, own, other):
    entries = energy.shape[1] * energy.shape[2] // WIDTH
    return pl.pallas_call(
        scale_kernel,
        out_shape=jax.ShapeDtypeStruct((2,) + own.shape, jnp.bfloat16),
        scratch_shapes=[pltpu.VMEM((entries, WIDTH), jnp.float32)] * 2,
        cost_estimate=pl.CostEstimate(flops=4 * 10**8, bytes_accessed=3 * 10**5, transcendentals=0),
        name="scale",
    )(energy, occupied, first, second, kpoint, own, other)


def product_kernel(side, place, rows, c0, c1, c2, c3, out):
    which = place[side]

    def columns(c, s):
        return c[s * L + which]

    left = jnp.concatenate(
        [
            jnp.concatenate([rows[(NEAR[s][j] + place[2]) % Z] for s in range(H)], axis=0)
            for j in range(3)
        ],
        axis=1,
    )
    right = jnp.concatenate(
        [
            jnp.concatenate([columns(c, s) for s in range(H)], axis=0)
            for c in (c0, c1, c2, c3)
        ],
        axis=1,
    )
    found = lax.dot_general(
        left, right, (((0,), (0,)), ((), ())), preferred_element_type=jnp.float32
    )
    for i in range(X):
        out[i] = found[:, i * WIDTH : (i + 1) * WIDTH].astype(out.dtype)


SMEM = pl.BlockSpec(memory_space=pltpu.SMEM)
VMEM = pl.BlockSpec(memory_space=pltpu.VMEM)


def product(side, place, rows, columns, dtype):
    return pl.pallas_call(
        functools.partial(product_kernel, side),
        out_shape=jax.ShapeDtypeStruct((X, 3 * WIDTH, WIDTH), dtype),
        in_specs=[SMEM] + [VMEM] * (1 + X),
        out_specs=VMEM,
        compiler_params=pltpu.CompilerParams(vmem_limit_bytes=16 * 2**20),
        cost_estimate=pl.CostEstimate(flops=4 * 10**8, bytes_accessed=3 * 10**6, transcendentals=0),
    )(place, rows, *columns)


def total_kernel(place, keep, taken, *outs):
    for r, out in enumerate(outs):
        i = (r + place[3]) % X
        out[...] = (keep[i] + taken[i].astype(jnp.float32)).astype(out.dtype)


def add_partner(place, keep, taken):
    return pl.pallas_call(
        total_kernel,
        out_shape=[jax.ShapeDtypeStruct(keep.shape[1:], jnp.bfloat16)] * X,
        in_specs=[SMEM, VMEM, VMEM],
        out_specs=[VMEM] * X,
        compiler_params=pltpu.CompilerParams(vmem_limit_bytes=8 * 2**20),
        name="total",
    )(place, keep, taken)


def assemble_kernel(place, f0, f1, f2, f3, out):
    for i, piece in enumerate((f0, f1, f2, f3)):
        t = place[4 + i]
        for j in range(3):
            out[j, t % 2, t // 2] = piece[j * WIDTH : (j + 1) * WIDTH, :].astype(jnp.float32)


def assemble(place, pieces):
    return pl.pallas_call(
        assemble_kernel,
        out_shape=jax.ShapeDtypeStruct((3, 2, 2, WIDTH, WIDTH), jnp.float32),
        in_specs=[SMEM] + [VMEM] * 4,
        out_specs=VMEM,
        compiler_params=pltpu.CompilerParams(vmem_limit_bytes=8 * 2**20),
        name="assemble",
    )(place, *pieces)


def blocks(pair_matrix, band_energy, occupation, pair_first, pair_second, pair_kpoint):
    pool, col = lax.axis_index("pool"), lax.axis_index("col")
    k, x, l = pool % K, col // (Z * L), col % L
    place = jnp.stack(
        [1 - k, k, 6 * (x // 2) + x % 2, 2 * l]
        + [(x - 2 * k - r) % X for r in range(X)]
    ).astype(jnp.int32)

    other = move(pair_matrix, lambda h, k, x, z, l: (h, k, x, z, 1 - l))
    sent = move(pair_matrix, spread)
    scaled = scaled_blocks(
        band_energy, occupation, pair_first, pair_second, pair_kpoint, pair_matrix, other
    )
    around = [scaled]
    for s in range(1, H):
        around.append(move(scaled, lambda h, k, x, z, l, s=s: (h - s, k, x, z, l)))
    both = jnp.concatenate(around, axis=0)
    columns = [both]
    for s in range(1, X):
        columns.append(move(both, lambda h, k, x, z, l, s=s: (h, k, x - s, z, l)))
    rows = lax.all_gather(sent, "col", axis=0, axis_index_groups=Z_GROUPS)

    give = product(0, place, rows, columns, jnp.bfloat16)
    taken = move(give, lambda h, k, x, z, l: (h, 1 - k, x, z, l))
    keep = product(1, place, rows, columns, jnp.float32)
    total = add_partner(place, keep, taken)
    home = []
    for r in range(X):
        home.append(
            move(
                total[r],
                lambda h, k, x, z, l, r=r: (h, x // 2, x + r + 2 * l, z, l ^ k),
            )
        )
    return assemble(place, home).reshape(-1, WIDTH)


def solution(mesh):
    return jax.shard_map(
        blocks,
        mesh=mesh,
        in_specs=(
            P("pool", "col"),
            P("pool", None, None),
            P("pool", None, None),
            P("pool", None),
            P("pool", None),
            P("pool", None),
        ),
        out_specs=P("pool", "col"),
        check_vma=False,
    )
```

```python
import functools

import jax
import jax.numpy as jnp
from jax import lax
from jax.experimental import pallas as pl
from jax.experimental.pallas import tpu as pltpu
from jax.sharding import PartitionSpec as P


H, K, X, Z, L = 4, 2, 4, 12, 2
COLS = X * Z * L
PAIRS, WIDTH = 256, 128
AXES = ("pool", "col")
NEAR = ((9, 5, 8), (11, 1, 6), (0, 2, 4), (10, 3, 7))


def at(h, k, x, z, l):
    return ((h % H) * K + k) * COLS + (x % X) * (Z * L) + (z % Z) * L + l


def table(f):
    return [
        (at(h, k, x, z, l), at(*f(h, k, x, z, l)))
        for h in range(H)
        for k in range(K)
        for x in range(X)
        for z in range(Z)
        for l in range(L)
    ]


def move(value, f):
    return lax.ppermute(value, AXES, table(f))


ROUNDS = (2, 1, 3, 0)


def turn(x, l):
    return l * (3 - 2 * (x % 2))


def spread(h, k, x, z, l):
    side, (j, a) = z // 6, divmod(z % 6, 2)
    return x, k, 2 * side + a, NEAR[(h - x) % H][j] + 6 * side + a, l


Z_GROUPS = [[x * Z * L + z * L + l for z in range(Z)] for x in range(X) for l in range(L)]


def scale_kernel(energy, occupied, first, second, kpoint, block, out, energies, filled):
    chunks = energy.shape[-1] // WIDTH
    kpts = energy.shape[-2]
    for c in range(chunks):
        part = pl.ds(c * WIDTH, WIDTH)
        energies[pl.ds(c * kpts, kpts), :] = energy[0, :, part]
        filled[pl.ds(c * kpts, kpts), :] = occupied[0, :, part].astype(jnp.float32)

    def pick(table_ref, band):
        entries = table_ref.shape[0]
        place = (band // WIDTH) * kpts + kpoint[...]
        spot = band % WIDTH
        pairs = band.shape[-1]
        one = (lax.broadcasted_iota(jnp.int32, (entries, pairs), 0) == place).astype(jnp.float32)
        found = lax.dot_general(
            table_ref[...],
            one,
            (((0,), (0,)), ((), ())),
            precision=lax.Precision.HIGHEST,
            preferred_element_type=jnp.float32,
        )
        keep = lax.broadcasted_iota(jnp.int32, (WIDTH, pairs), 0) == spot
        return jnp.sum(jnp.where(keep, found, 0.0), axis=0, keepdims=True)

    a, b = first[...], second[...]
    gap = jnp.abs(pick(energies, b) - pick(energies, a))
    change = pick(filled, a) - pick(filled, b)
    weight = 2.0 * change / (1.0 + gap)
    for i in range(PAIRS // WIDTH):
        rows = pl.ds(i * WIDTH, WIDTH)
        factor = jnp.broadcast_to(weight[:, i * WIDTH : (i + 1) * WIDTH], (WIDTH, WIDTH)).T
        out[rows, :] = (block[rows, :].astype(jnp.float32) * factor).astype(jnp.bfloat16)


def scaled_block(energy, occupied, first, second, kpoint, block):
    entries = energy.shape[1] * energy.shape[2] // WIDTH
    return pl.pallas_call(
        scale_kernel,
        out_shape=jax.ShapeDtypeStruct(block.shape, jnp.bfloat16),
        scratch_shapes=[pltpu.VMEM((entries, WIDTH), jnp.float32)] * 2,
        cost_estimate=pl.CostEstimate(flops=4 * 10**8, bytes_accessed=3 * 10**5, transcendentals=0),
        name="scale",
    )(energy, occupied, first, second, kpoint, block)


def product_kernel(side, place, rows, c0, c1, c2, c3, out):
    which = place[side]
    left = jnp.concatenate(
        [
            jnp.concatenate([rows[(NEAR[s][j] + place[2]) % Z] for s in range(H)], axis=0)
            for j in range(3)
        ],
        axis=1,
    )
    right = jnp.concatenate([c[which] for c in (c0, c1, c2, c3)], axis=1)
    found = lax.dot_general(
        left, right, (((0,), (0,)), ((), ())), preferred_element_type=jnp.float32
    )
    for i in range(X):
        out[i] = found[:, i * WIDTH : (i + 1) * WIDTH].astype(out.dtype)


SMEM = pl.BlockSpec(memory_space=pltpu.SMEM)
VMEM = pl.BlockSpec(memory_space=pltpu.VMEM)


def product(side, place, rows, columns, dtype):
    return pl.pallas_call(
        functools.partial(product_kernel, side),
        out_shape=jax.ShapeDtypeStruct((X, 3 * WIDTH, WIDTH), dtype),
        in_specs=[SMEM] + [VMEM] * (1 + X),
        out_specs=VMEM,
        compiler_params=pltpu.CompilerParams(vmem_limit_bytes=16 * 2**20),
        cost_estimate=pl.CostEstimate(flops=4 * 10**8, bytes_accessed=3 * 10**6, transcendentals=0),
    )(place, rows, *columns)


def total_kernel(place, keep, taken, *outs):
    for r, out in enumerate(outs):
        i = (ROUNDS[r] + place[3]) % X
        out[...] = (keep[i] + taken[i].astype(jnp.float32)).astype(out.dtype)


def add_partner(place, keep, taken):
    return pl.pallas_call(
        total_kernel,
        out_shape=[jax.ShapeDtypeStruct(keep.shape[1:], jnp.bfloat16)] * X,
        in_specs=[SMEM, VMEM, VMEM],
        out_specs=[VMEM] * X,
        compiler_params=pltpu.CompilerParams(vmem_limit_bytes=8 * 2**20),
        name="total",
    )(place, keep, taken)


def settle_kernel(start, count, place, *refs):
    pieces, (out, wide, sems) = refs[:count], refs[-3:]
    copies = []
    for i, piece in enumerate(pieces):
        t = place[4 + start + i]
        b = t // 2
        a = (t + b) % 2
        for j in range(3):
            wide[i, j] = piece[j * WIDTH : (j + 1) * WIDTH, :].astype(jnp.float32)
            copies.append(
                pltpu.make_async_copy(wide.at[i, j], out.at[j, a, b], sems.at[i, j])
            )
            copies[-1].start()
    for copy in copies:
        copy.wait()


def settle(place, start, pieces, out=None):
    count = len(pieces)
    given = [] if out is None else [out]
    return pl.pallas_call(
        functools.partial(settle_kernel, start, count),
        out_shape=jax.ShapeDtypeStruct((3, 2, 2, WIDTH, WIDTH), jnp.float32),
        in_specs=[SMEM] + [VMEM] * count + [pl.BlockSpec(memory_space=pl.ANY)] * len(given),
        out_specs=pl.BlockSpec(memory_space=pl.ANY),
        scratch_shapes=[
            pltpu.VMEM((count, 3, WIDTH, WIDTH), jnp.float32),
            pltpu.SemaphoreType.DMA((count, 3)),
        ],
        input_output_aliases={1 + count: 0} if given else {},
        compiler_params=pltpu.CompilerParams(vmem_limit_bytes=8 * 2**20),
    )(place, *pieces, *given)


def blocks(pair_matrix, band_energy, occupation, pair_first, pair_second, pair_kpoint):
    pool, col = lax.axis_index("pool"), lax.axis_index("col")
    k, x, l = pool % K, col // (Z * L), col % L
    place = jnp.stack(
        [1 - k, k, 6 * (x // 2) + x % 2, turn(x, l)]
        + [(x - 2 * k - r) % X for r in ROUNDS]
    ).astype(jnp.int32)

    around = []
    for s in range(1, H):
        around.append(move(pair_matrix, lambda h, k, x, z, l, s=s: (h - s, k, x, z, l)))
    scaled = scaled_block(
        band_energy, occupation, pair_first, pair_second, pair_kpoint, pair_matrix
    )
    sent = move(scaled, spread)
    own = jnp.concatenate([pair_matrix] + around, axis=0)
    other = move(own, lambda h, k, x, z, l: (h, k, x, z, 1 - l))
    both = jnp.stack([own, other])
    columns = [both]
    for s in range(1, X):
        columns.append(move(both, lambda h, k, x, z, l, s=s: (h, k, x - s, z, l)))
    rows = lax.all_gather(sent, "col", axis=0, axis_index_groups=Z_GROUPS)

    give = product(0, place, rows, columns, jnp.bfloat16)
    taken = move(give, lambda h, k, x, z, l: (h, 1 - k, x, z, l))
    keep = product(1, place, rows, columns, jnp.float32)
    total = add_partner(place, keep, taken)
    home = []
    for r in range(X):
        home.append(
            move(
                total[r],
                lambda h, k, x, z, l, r=r: (
                    h, x // 2, x + ROUNDS[r] + turn(x, l), z, l ^ k
                ),
            )
        )
    most = settle(place, 0, home[:3])
    return settle(place, 3, home[3:], most).reshape(-1, WIDTH)


def solution(mesh):
    return jax.shard_map(
        blocks,
        mesh=mesh,
        in_specs=(
            P("pool", "col"),
            P("pool", None, None),
            P("pool", None, None),
            P("pool", None),
            P("pool", None),
            P("pool", None),
        ),
        out_specs=P("pool", "col"),
        check_vma=False,
    )
```

```python
import functools

import jax
import jax.numpy as jnp
from jax import lax
from jax.experimental import pallas as pl
from jax.experimental.pallas import tpu as pltpu
from jax.sharding import PartitionSpec as P


H, K, X, Z, L = 4, 2, 4, 12, 2
COLS = X * Z * L
PAIRS, WIDTH = 256, 128
AXES = ("pool", "col")
SHIFT = (2, 1, 0, 3)


def at(h, k, x, z, l):
    return ((h % H) * K + k) * COLS + (x % X) * (Z * L) + (z % Z) * L + l


def table(f):
    return [
        (at(h, k, x, z, l), at(*f(h, k, x, z, l)))
        for h in range(H)
        for k in range(K)
        for x in range(X)
        for z in range(Z)
        for l in range(L)
    ]


def move(value, f):
    return lax.ppermute(value, AXES, table(f))


Z_GROUPS = [[x * Z * L + z * L + l for z in range(Z)] for x in range(X) for l in range(L)]


def scale_kernel(energy, occupied, first, second, kpoint, block, out, energies, filled):
    chunks = energy.shape[-1] // WIDTH
    kpts = energy.shape[-2]
    for c in range(chunks):
        part = pl.ds(c * WIDTH, WIDTH)
        energies[pl.ds(c * kpts, kpts), :] = energy[0, :, part]
        filled[pl.ds(c * kpts, kpts), :] = occupied[0, :, part].astype(jnp.float32)

    def pick(table_ref, band):
        entries = table_ref.shape[0]
        place = (band // WIDTH) * kpts + kpoint[...]
        spot = band % WIDTH
        pairs = band.shape[-1]
        one = (lax.broadcasted_iota(jnp.int32, (entries, pairs), 0) == place).astype(jnp.float32)
        found = lax.dot_general(
            table_ref[...],
            one,
            (((0,), (0,)), ((), ())),
            precision=lax.Precision.HIGHEST,
            preferred_element_type=jnp.float32,
        )
        keep = lax.broadcasted_iota(jnp.int32, (WIDTH, pairs), 0) == spot
        return jnp.sum(jnp.where(keep, found, 0.0), axis=0, keepdims=True)

    a, b = first[...], second[...]
    gap = jnp.abs(pick(energies, b) - pick(energies, a))
    change = pick(filled, a) - pick(filled, b)
    weight = 2.0 * change / (1.0 + gap)
    for i in range(PAIRS // WIDTH):
        rows = pl.ds(i * WIDTH, WIDTH)
        factor = jnp.broadcast_to(weight[:, i * WIDTH : (i + 1) * WIDTH], (WIDTH, WIDTH)).T
        out[rows, :] = (block[rows, :].astype(jnp.float32) * factor).astype(jnp.bfloat16)


def scaled_block(energy, occupied, first, second, kpoint, block):
    entries = energy.shape[1] * energy.shape[2] // WIDTH
    return pl.pallas_call(
        scale_kernel,
        out_shape=jax.ShapeDtypeStruct(block.shape, jnp.bfloat16),
        scratch_shapes=[pltpu.VMEM((entries, WIDTH), jnp.float32)] * 2,
        cost_estimate=pl.CostEstimate(flops=4 * 10**8, bytes_accessed=3 * 10**5, transcendentals=0),
        name="scale",
    )(energy, occupied, first, second, kpoint, block)


def join_kernel(*refs):
    for i, part in enumerate(refs[:-1]):
        refs[-1][i] = part[...]


def join(parts):
    return pl.pallas_call(
        join_kernel,
        out_shape=jax.ShapeDtypeStruct((len(parts),) + parts[0].shape, parts[0].dtype),
        in_specs=[pl.BlockSpec(memory_space=pltpu.VMEM)] * len(parts),
        out_specs=pl.BlockSpec(memory_space=pltpu.VMEM),
        compiler_params=pltpu.CompilerParams(vmem_limit_bytes=8 * 2**20),
    )(*parts)


def product_kernel(side, place, rows, c0, c1, c2, c3, out):
    which = place[side]
    left = jnp.concatenate(
        [
            jnp.concatenate([rows[3 * ((place[2] + SHIFT[s]) % H) + j] for s in range(H)], axis=0)
            for j in range(3)
        ],
        axis=1,
    )
    right = jnp.concatenate([c[which] for c in (c0, c1, c2, c3)], axis=1)
    found = lax.dot_general(
        left, right, (((0,), (0,)), ((), ())), preferred_element_type=jnp.float32
    )
    for i in range(X):
        out[i] = found[:, i * WIDTH : (i + 1) * WIDTH].astype(out.dtype)


SMEM = pl.BlockSpec(memory_space=pltpu.SMEM)
VMEM = pl.BlockSpec(memory_space=pltpu.VMEM)


def product(side, place, rows, columns, dtype):
    return pl.pallas_call(
        functools.partial(product_kernel, side),
        out_shape=jax.ShapeDtypeStruct((X, 3 * WIDTH, WIDTH), dtype),
        in_specs=[SMEM] + [VMEM] * (1 + X),
        out_specs=VMEM,
        compiler_params=pltpu.CompilerParams(vmem_limit_bytes=16 * 2**20),
        cost_estimate=pl.CostEstimate(flops=4 * 10**8, bytes_accessed=3 * 10**6, transcendentals=0),
    )(place, rows, *columns)


def total_kernel(place, keep, taken, *outs):
    for r, out in enumerate(outs):
        i = (r + place[3]) % X
        out[...] = (keep[i] + taken[i].astype(jnp.float32)).astype(out.dtype)


def add_partner(place, keep, taken):
    return pl.pallas_call(
        total_kernel,
        out_shape=[jax.ShapeDtypeStruct(keep.shape[1:], jnp.bfloat16)] * X,
        in_specs=[SMEM, VMEM, VMEM],
        out_specs=[VMEM] * X,
        compiler_params=pltpu.CompilerParams(vmem_limit_bytes=8 * 2**20),
        name="total",
    )(place, keep, taken)


def assemble_kernel(place, f0, f1, f2, f3, out):
    for i, piece in enumerate((f0, f1, f2, f3)):
        t = place[4 + i]
        for j in range(3):
            out[t % 2, j, t // 2] = piece[j * WIDTH : (j + 1) * WIDTH, :].astype(jnp.float32)


def assemble(place, pieces):
    return pl.pallas_call(
        assemble_kernel,
        out_shape=jax.ShapeDtypeStruct((2, 3, 2, WIDTH, WIDTH), jnp.float32),
        in_specs=[SMEM] + [VMEM] * 4,
        out_specs=VMEM,
        compiler_params=pltpu.CompilerParams(vmem_limit_bytes=8 * 2**20),
        name="assemble",
    )(place, *pieces)


def blocks(pair_matrix, band_energy, occupation, pair_first, pair_second, pair_kpoint):
    pool, col = lax.axis_index("pool"), lax.axis_index("col")
    k, x, l = pool % K, col // (Z * L), col % L
    place = jnp.stack(
        [1 - k, k, x, 2 * l] + [(x - 2 * k - r) % X for r in range(X)]
    ).astype(jnp.int32)

    around = []
    for s in range(1, H):
        around.append(move(pair_matrix, lambda h, k, x, z, l, s=s: (h - s, k, x, z, l)))
    scaled = scaled_block(
        band_energy, occupation, pair_first, pair_second, pair_kpoint, pair_matrix
    )
    sent = move(
        scaled,
        lambda h, k, x, z, l: (x, k, z // 3, z + 3 * SHIFT[(h - x) % H], l),
    )
    own = join([pair_matrix] + around).reshape(H * PAIRS, WIDTH)
    other = move(own, lambda h, k, x, z, l: (h, k, x, z, 1 - l))
    both = join([own, other])
    columns = [both]
    for s in range(1, X):
        columns.append(move(both, lambda h, k, x, z, l, s=s: (h, k, x - s, z, l)))
    rows = lax.all_gather(sent, "col", axis=0, axis_index_groups=Z_GROUPS)

    give = product(0, place, rows, columns, jnp.bfloat16)
    taken = move(give, lambda h, k, x, z, l: (h, 1 - k, x, z, l))
    keep = product(1, place, rows, columns, jnp.float32)
    total = add_partner(place, keep, taken)
    home = []
    for r in range(X):
        home.append(
            move(
                total[r],
                lambda h, k, x, z, l, r=r: (h, x // 2, x + r + 2 * l, z, l ^ k),
            )
        )
    return assemble(place, home).reshape(-1, WIDTH)


def solution(mesh):
    return jax.shard_map(
        blocks,
        mesh=mesh,
        in_specs=(
            P("pool", "col"),
            P("pool", None, None),
            P("pool", None, None),
            P("pool", None),
            P("pool", None),
            P("pool", None),
        ),
        out_specs=P("pool", "col"),
        check_vma=False,
    )
```

```python
import functools

import jax
import jax.numpy as jnp
from jax import lax
from jax.experimental import pallas as pl
from jax.experimental.pallas import tpu as pltpu
from jax.sharding import PartitionSpec as P


H, K, X, Z, L = 4, 2, 4, 12, 2
COLS = X * Z * L
PAIRS, WIDTH = 256, 128
AXES = ("pool", "col")
SHIFT = (2, 1, 0, 3)


def at(h, k, x, z, l):
    return ((h % H) * K + k) * COLS + (x % X) * (Z * L) + (z % Z) * L + l


def table(f):
    return [
        (at(h, k, x, z, l), at(*f(h, k, x, z, l)))
        for h in range(H)
        for k in range(K)
        for x in range(X)
        for z in range(Z)
        for l in range(L)
    ]


def move(value, f):
    return lax.ppermute(value, AXES, table(f))


def half(k, z):
    return k ^ (z % 2)


Z_GROUPS = [
    [at(h, half(n, z), x, z, l) for z in range(Z)]
    for h in range(H)
    for n in range(K)
    for x in range(X)
    for l in range(L)
]


def spread(h, k, x, z, l):
    to = (z + 3 * SHIFT[(h - x) % H]) % Z
    return x, half(k, to), z // 3, to, l


def scale_kernel(energy, occupied, first, second, kpoint, block, out, energies, filled):
    chunks = energy.shape[-1] // WIDTH
    kpts = energy.shape[-2]
    for c in range(chunks):
        part = pl.ds(c * WIDTH, WIDTH)
        energies[pl.ds(c * kpts, kpts), :] = energy[0, :, part]
        filled[pl.ds(c * kpts, kpts), :] = occupied[0, :, part].astype(jnp.float32)

    def pick(table_ref, band):
        entries = table_ref.shape[0]
        place = (band // WIDTH) * kpts + kpoint[...]
        spot = band % WIDTH
        pairs = band.shape[-1]
        one = (lax.broadcasted_iota(jnp.int32, (entries, pairs), 0) == place).astype(jnp.float32)
        found = lax.dot_general(
            table_ref[...],
            one,
            (((0,), (0,)), ((), ())),
            precision=lax.Precision.HIGHEST,
            preferred_element_type=jnp.float32,
        )
        keep = lax.broadcasted_iota(jnp.int32, (WIDTH, pairs), 0) == spot
        return jnp.sum(jnp.where(keep, found, 0.0), axis=0, keepdims=True)

    a, b = first[...], second[...]
    gap = jnp.abs(pick(energies, b) - pick(energies, a))
    change = pick(filled, a) - pick(filled, b)
    weight = 2.0 * change / (1.0 + gap)
    for i in range(PAIRS // WIDTH):
        rows = pl.ds(i * WIDTH, WIDTH)
        factor = jnp.broadcast_to(weight[:, i * WIDTH : (i + 1) * WIDTH], (WIDTH, WIDTH)).T
        out[rows, :] = (block[rows, :].astype(jnp.float32) * factor).astype(jnp.bfloat16)


def scaled_block(energy, occupied, first, second, kpoint, block):
    entries = energy.shape[1] * energy.shape[2] // WIDTH
    return pl.pallas_call(
        scale_kernel,
        out_shape=jax.ShapeDtypeStruct(block.shape, jnp.bfloat16),
        scratch_shapes=[pltpu.VMEM((entries, WIDTH), jnp.float32)] * 2,
        cost_estimate=pl.CostEstimate(flops=4 * 10**8, bytes_accessed=3 * 10**5, transcendentals=0),
        name="scale",
    )(energy, occupied, first, second, kpoint, block)


def product_kernel(side, place, rows, c0, c1, c2, c3, out):
    which = place[side]
    left = jnp.concatenate(
        [
            jnp.concatenate([rows[3 * ((place[2] + SHIFT[s]) % H) + j] for s in range(H)], axis=0)
            for j in range(3)
        ],
        axis=1,
    )
    right = jnp.concatenate([c[which] for c in (c0, c1, c2, c3)], axis=1)
    found = lax.dot_general(
        left, right, (((0,), (0,)), ((), ())), preferred_element_type=jnp.float32
    )
    for i in range(X):
        out[i] = found[:, i * WIDTH : (i + 1) * WIDTH].astype(out.dtype)


SMEM = pl.BlockSpec(memory_space=pltpu.SMEM)
VMEM = pl.BlockSpec(memory_space=pltpu.VMEM)


def product(side, place, rows, columns, dtype):
    return pl.pallas_call(
        functools.partial(product_kernel, side),
        out_shape=jax.ShapeDtypeStruct((X, 3 * WIDTH, WIDTH), dtype),
        in_specs=[SMEM] + [VMEM] * (1 + X),
        out_specs=VMEM,
        compiler_params=pltpu.CompilerParams(vmem_limit_bytes=16 * 2**20),
        cost_estimate=pl.CostEstimate(flops=4 * 10**8, bytes_accessed=3 * 10**6, transcendentals=0),
    )(place, rows, *columns)


def total_kernel(place, keep, taken, *outs):
    for r, out in enumerate(outs):
        i = (r + place[3]) % X
        out[...] = (keep[i] + taken[i].astype(jnp.float32)).astype(out.dtype)


def add_partner(place, keep, taken):
    return pl.pallas_call(
        total_kernel,
        out_shape=[jax.ShapeDtypeStruct(keep.shape[1:], jnp.bfloat16)] * X,
        in_specs=[SMEM, VMEM, VMEM],
        out_specs=[VMEM] * X,
        compiler_params=pltpu.CompilerParams(vmem_limit_bytes=8 * 2**20),
        name="total",
    )(place, keep, taken)


def assemble_kernel(place, f0, f1, f2, f3, out):
    for i, piece in enumerate((f0, f1, f2, f3)):
        t = place[4 + i]
        for j in range(3):
            out[t % 2, j, t // 2] = piece[j * WIDTH : (j + 1) * WIDTH, :].astype(jnp.float32)


def assemble(place, pieces):
    return pl.pallas_call(
        assemble_kernel,
        out_shape=jax.ShapeDtypeStruct((2, 3, 2, WIDTH, WIDTH), jnp.float32),
        in_specs=[SMEM] + [VMEM] * 4,
        out_specs=VMEM,
        compiler_params=pltpu.CompilerParams(vmem_limit_bytes=8 * 2**20),
        name="assemble",
    )(place, *pieces)


def blocks(pair_matrix, band_energy, occupation, pair_first, pair_second, pair_kpoint):
    pool, col = lax.axis_index("pool"), lax.axis_index("col")
    k, x, l = pool % K, col // (Z * L), col % L
    place = jnp.stack(
        [1 - k, k, x, 2 * l] + [(x - 2 * k - r) % X for r in range(X)]
    ).astype(jnp.int32)

    around = []
    for s in range(H):
        around.append(move(pair_matrix, lambda h, k, x, z, l, s=s: (h - s, half(k, z), x, z, l)))
    scaled = scaled_block(
        band_energy, occupation, pair_first, pair_second, pair_kpoint, pair_matrix
    )
    sent = move(scaled, spread)
    own = jnp.concatenate(around, axis=0)
    other = move(own, lambda h, k, x, z, l: (h, k, x, z, 1 - l))
    both = jnp.stack([own, other])
    columns = [both]
    for s in range(1, X):
        columns.append(move(both, lambda h, k, x, z, l, s=s: (h, k, x - s, z, l)))
    rows = lax.all_gather(sent, AXES, axis=0, axis_index_groups=Z_GROUPS)

    give = product(0, place, rows, columns, jnp.bfloat16)
    taken = move(give, lambda h, k, x, z, l: (h, 1 - k, x, z, l))
    keep = product(1, place, rows, columns, jnp.float32)
    total = add_partner(place, keep, taken)
    home = []
    for r in range(X):
        home.append(
            move(
                total[r],
                lambda h, k, x, z, l, r=r: (h, x // 2, x + r + 2 * l, z, l ^ k),
            )
        )
    return assemble(place, home).reshape(-1, WIDTH)


def solution(mesh):
    return jax.shard_map(
        blocks,
        mesh=mesh,
        in_specs=(
            P("pool", "col"),
            P("pool", None, None),
            P("pool", None, None),
            P("pool", None),
            P("pool", None),
            P("pool", None),
        ),
        out_specs=P("pool", "col"),
        check_vma=False,
    )
```

```python
import functools

import jax
import jax.numpy as jnp
from jax import lax
from jax.experimental import pallas as pl
from jax.experimental.pallas import tpu as pltpu
from jax.sharding import PartitionSpec as P


H, K, X, Z, L = 4, 2, 4, 12, 2
COLS = X * Z * L
PAIRS, WIDTH = 256, 128
AXES = ("pool", "col")
NEAR = ((9, 5, 8), (11, 1, 6), (0, 2, 4), (10, 3, 7))


def at(h, k, x, z, l):
    return ((h % H) * K + k) * COLS + (x % X) * (Z * L) + (z % Z) * L + l


def table(f):
    return [
        (at(h, k, x, z, l), at(*f(h, k, x, z, l)))
        for h in range(H)
        for k in range(K)
        for x in range(X)
        for z in range(Z)
        for l in range(L)
    ]


def move(value, f):
    return lax.ppermute(value, AXES, table(f))


def spread(h, k, x, z, l):
    side, (j, a) = z // 6, divmod(z % 6, 2)
    return x, k, 2 * side + a, NEAR[(h - x) % H][j] + 6 * side + a, l


H_GROUPS = [[h * K + k for h in range(H)] for k in range(K)]
Z_GROUPS = [[x * Z * L + z * L + l for z in range(Z)] for x in range(X) for l in range(L)]


def scale_kernel(energy, occupied, first, second, kpoint, block, out, energies, filled):
    chunks = energy.shape[-1] // WIDTH
    kpts = energy.shape[-2]
    for c in range(chunks):
        part = pl.ds(c * WIDTH, WIDTH)
        energies[pl.ds(c * kpts, kpts), :] = energy[0, :, part]
        filled[pl.ds(c * kpts, kpts), :] = occupied[0, :, part].astype(jnp.float32)

    def pick(table_ref, band):
        entries = table_ref.shape[0]
        place = (band // WIDTH) * kpts + kpoint[...]
        spot = band % WIDTH
        pairs = band.shape[-1]
        one = (lax.broadcasted_iota(jnp.int32, (entries, pairs), 0) == place).astype(jnp.float32)
        found = lax.dot_general(
            table_ref[...],
            one,
            (((0,), (0,)), ((), ())),
            precision=lax.Precision.HIGHEST,
            preferred_element_type=jnp.float32,
        )
        keep = lax.broadcasted_iota(jnp.int32, (WIDTH, pairs), 0) == spot
        return jnp.sum(jnp.where(keep, found, 0.0), axis=0, keepdims=True)

    a, b = first[...], second[...]
    gap = jnp.abs(pick(energies, b) - pick(energies, a))
    change = pick(filled, a) - pick(filled, b)
    weight = 2.0 * change / (1.0 + gap)
    for i in range(PAIRS // WIDTH):
        rows = pl.ds(i * WIDTH, WIDTH)
        factor = jnp.broadcast_to(weight[:, i * WIDTH : (i + 1) * WIDTH], (WIDTH, WIDTH)).T
        out[rows, :] = (block[rows, :].astype(jnp.float32) * factor).astype(jnp.bfloat16)


def scaled_block(energy, occupied, first, second, kpoint, block):
    entries = energy.shape[1] * energy.shape[2] // WIDTH
    return pl.pallas_call(
        scale_kernel,
        out_shape=jax.ShapeDtypeStruct(block.shape, jnp.bfloat16),
        scratch_shapes=[pltpu.VMEM((entries, WIDTH), jnp.float32)] * 2,
        cost_estimate=pl.CostEstimate(flops=4 * 10**8, bytes_accessed=3 * 10**5, transcendentals=0),
        name="scale",
    )(energy, occupied, first, second, kpoint, block)


def join_kernel(*refs):
    for i, part in enumerate(refs[:-1]):
        refs[-1][i] = part[...]


def join(parts):
    return pl.pallas_call(
        join_kernel,
        out_shape=jax.ShapeDtypeStruct((len(parts),) + parts[0].shape, parts[0].dtype),
        in_specs=[pl.BlockSpec(memory_space=pltpu.VMEM)] * len(parts),
        out_specs=pl.BlockSpec(memory_space=pltpu.VMEM),
        compiler_params=pltpu.CompilerParams(vmem_limit_bytes=8 * 2**20),
    )(*parts)


def product_kernel(side, place, rows, c0, c1, c2, c3, out):
    which = place[side]

    def columns(c, s):
        start = pl.multiple_of(((place[8] + s) % H) * PAIRS, PAIRS)
        return c[which, pl.ds(start, PAIRS), :]

    left = jnp.concatenate(
        [
            jnp.concatenate([rows[(NEAR[s][j] + place[2]) % Z] for s in range(H)], axis=0)
            for j in range(3)
        ],
        axis=1,
    )
    right = jnp.concatenate(
        [
            jnp.concatenate([columns(c, s) for s in range(H)], axis=0)
            for c in (c0, c1, c2, c3)
        ],
        axis=1,
    )
    found = lax.dot_general(
        left, right, (((0,), (0,)), ((), ())), preferred_element_type=jnp.float32
    )
    for i in range(X):
        out[i] = found[:, i * WIDTH : (i + 1) * WIDTH].astype(out.dtype)


SMEM = pl.BlockSpec(memory_space=pltpu.SMEM)
VMEM = pl.BlockSpec(memory_space=pltpu.VMEM)


def product(side, place, rows, columns, dtype):
    return pl.pallas_call(
        functools.partial(product_kernel, side),
        out_shape=jax.ShapeDtypeStruct((X, 3 * WIDTH, WIDTH), dtype),
        in_specs=[SMEM] + [VMEM] * (1 + X),
        out_specs=VMEM,
        compiler_params=pltpu.CompilerParams(vmem_limit_bytes=16 * 2**20),
        cost_estimate=pl.CostEstimate(flops=4 * 10**8, bytes_accessed=3 * 10**6, transcendentals=0),
    )(place, rows, *columns)


def total_kernel(place, keep, taken, *outs):
    for r, out in enumerate(outs):
        i = (r + place[3]) % X
        out[...] = (keep[i] + taken[i].astype(jnp.float32)).astype(out.dtype)


def add_partner(place, keep, taken):
    return pl.pallas_call(
        total_kernel,
        out_shape=[jax.ShapeDtypeStruct(keep.shape[1:], jnp.bfloat16)] * X,
        in_specs=[SMEM, VMEM, VMEM],
        out_specs=[VMEM] * X,
        compiler_params=pltpu.CompilerParams(vmem_limit_bytes=8 * 2**20),
        name="total",
    )(place, keep, taken)


def assemble_kernel(place, f0, f1, f2, f3, out):
    for i, piece in enumerate((f0, f1, f2, f3)):
        t = place[4 + i]
        for j in range(3):
            out[j, t % 2, t // 2] = piece[j * WIDTH : (j + 1) * WIDTH, :].astype(jnp.float32)


def assemble(place, pieces):
    return pl.pallas_call(
        assemble_kernel,
        out_shape=jax.ShapeDtypeStruct((3, 2, 2, WIDTH, WIDTH), jnp.float32),
        in_specs=[SMEM] + [VMEM] * 4,
        out_specs=VMEM,
        compiler_params=pltpu.CompilerParams(vmem_limit_bytes=8 * 2**20),
        name="assemble",
    )(place, *pieces)


def blocks(pair_matrix, band_energy, occupation, pair_first, pair_second, pair_kpoint):
    pool, col = lax.axis_index("pool"), lax.axis_index("col")
    k, x, l = pool % K, col // (Z * L), col % L
    place = jnp.stack(
        [1 - k, k, 6 * (x // 2) + x % 2, 2 * l]
        + [(x - 2 * k - r) % X for r in range(X)]
        + [pool // K]
    ).astype(jnp.int32)

    own = lax.all_gather(
        pair_matrix, "pool", axis=0, tiled=True, axis_index_groups=H_GROUPS
    )
    scaled = scaled_block(
        band_energy, occupation, pair_first, pair_second, pair_kpoint, pair_matrix
    )
    sent = move(scaled, spread)
    other = move(own, lambda h, k, x, z, l: (h, k, x, z, 1 - l))
    both = join([own, other])
    columns = [both]
    for s in range(1, X):
        columns.append(move(both, lambda h, k, x, z, l, s=s: (h, k, x - s, z, l)))
    rows = lax.all_gather(sent, "col", axis=0, axis_index_groups=Z_GROUPS)

    give = product(0, place, rows, columns, jnp.bfloat16)
    taken = move(give, lambda h, k, x, z, l: (h, 1 - k, x, z, l))
    keep = product(1, place, rows, columns, jnp.float32)
    total = add_partner(place, keep, taken)
    home = []
    for r in range(X):
        home.append(
            move(
                total[r],
                lambda h, k, x, z, l, r=r: (h, x // 2, x + r + 2 * l, z, l ^ k),
            )
        )
    return assemble(place, home).reshape(-1, WIDTH)


def solution(mesh):
    return jax.shard_map(
        blocks,
        mesh=mesh,
        in_specs=(
            P("pool", "col"),
            P("pool", None, None),
            P("pool", None, None),
            P("pool", None),
            P("pool", None),
            P("pool", None),
        ),
        out_specs=P("pool", "col"),
        check_vma=False,
    )
```
